128 devices in a mesh: width: 16 (over x_lo, z, core), token: 4 (over y), query: 2 (over x_hi).
Axes of the slice: x: 4 (x_hi: 2, x_lo: 2; x = x_hi * 2 + x_lo), y: 4, z: 4, core: 2. Of those that a mesh axis runs over, the one named last changes fastest.
Arguments:
- layer_inputs: bfloat16 [1536, 8192], P(('token', 'query'), 'width'), may hold values from -20 to 20
- out_grads: bfloat16 [1536, 8192], P(('token', 'query'), 'width'), may hold values from -20 to 20
- basis_in: bfloat16 [8192, 8192], P(None, 'width'), may hold values from -0.125 to 0.125
- basis_out: bfloat16 [8192, 8192], P(None, 'width'), may hold values from -0.125 to 0.125
- query_in: bfloat16 [256, 32, 8192], P('query', None, 'width'), may hold values from -0.03125 to 0.03125
- query_out: bfloat16 [256, 32, 8192], P('query', None, 'width'), may hold values from -0.03125 to 0.03125
Outputs:
- scores: float32 [256, 1536], P('query', 'token')
The draws below stay inside these ranges and needn't reach their ends.
All inputs are finite; a program needn't handle non-finite values.
Results may differ from the reference program's by a relative error of at most 0.0003.
Values may be sent and summed in bfloat16 or wider, within the bound.
A program may use at most 128 MiB of HBM per device.

```python
import math
import jax
import jax.numpy as jnp
from jax import lax

D = 8192
RANK = 32
TOKENS = 1536
QUERIES = 256


def activation_draw(key, salt):
    first = jax.random.fold_in(jax.random.fold_in(key, salt), 0)
    base = jnp.clip(jax.random.normal(first, (TOKENS, D), jnp.float32), -4.0, 4.0)
    position = jnp.arange(TOKENS, dtype=jnp.float32) / TOKENS
    factor = 0.6 + 1.2 * position
    return (base * factor[:, None]).astype(jnp.bfloat16)


def basis_draw(key, salt):
    first, second = jax.random.split(jax.random.fold_in(key, salt))
    base = jnp.clip(jax.random.normal(first, (D, D), jnp.float32), -4.0, 4.0)
    column_scale = jnp.exp(jax.random.uniform(second, (D,), jnp.float32, math.log(0.3), math.log(3.0)))
    values = base * column_scale[None, :] / math.sqrt(D)
    return jnp.clip(values, -0.125, 0.125).astype(jnp.bfloat16)


def draw_layer_inputs(key, part):
    return activation_draw(key, 11)


def draw_out_grads(key, part):
    return activation_draw(key, 23)


def draw_basis_in(key, part):
    return basis_draw(key, 37)


def draw_basis_out(key, part):
    return basis_draw(key, 41)


def steps_of(own_key, extent, cuts, smallest, high):
    gain = 1.0
    for axis_at, blocks in cuts:
        steps = jax.random.uniform(jax.random.fold_in(jax.random.fold_in(own_key, 6), axis_at), (blocks,), jnp.float32, smallest / len(cuts), high / len(cuts))
        gain = gain * jnp.repeat(jnp.exp(steps), extent[axis_at] // blocks).reshape((-1,) + (1,) * (len(extent) - 1 - axis_at))
    return gain


def scatter_about(own_key, dims, width, reach, cuts=(), kind=jnp.bfloat16):
    entries = jax.random.normal(own_key, dims, jnp.float32) * width
    if len(cuts) > 0:
        entries = steps_of(own_key, dims, cuts, -0.22, 0.18) * entries
    return jnp.clip(entries, min=-reach, max=reach).astype(kind)


def setup_inputs(seed: int = 0) -> dict:
    seeds = jax.random.split(jax.random.key(seed), 7)
    layer_inputs = draw_layer_inputs(jax.random.fold_in(seeds[6], 71), 0)
    out_grads = draw_out_grads(jax.random.fold_in(seeds[6], 71), 0)
    basis_in = draw_basis_in(jax.random.fold_in(seeds[6], 71), 0)
    basis_out = draw_basis_out(jax.random.fold_in(seeds[6], 71), 0)
    query_in = scatter_about(seeds[4], (QUERIES, RANK, D), (4 * D) ** -0.5, 0.03125, ((0, 2), (2, 16)))
    query_out = scatter_about(seeds[5], (QUERIES, RANK, D), (4 * D) ** -0.5, 0.03125, ((0, 2), (2, 16)))
    return {"layer_inputs": layer_inputs, "out_grads": out_grads, "basis_in": basis_in, "basis_out": basis_out, "query_in": query_in, "query_out": query_out}


damping = 0.1


def reference(layer_inputs, out_grads, basis_in, basis_out, query_in, query_out):
    rotated_in = jnp.dot(layer_inputs, basis_in, preferred_element_type=jnp.float32)
    rotated_out = jnp.dot(out_grads, basis_out, preferred_element_type=jnp.float32)
    eigen_in = jnp.sum(rotated_in * rotated_in, axis=0) / TOKENS
    eigen_out = jnp.sum(rotated_out * rotated_out, axis=0) / TOKENS
    scaled_in = rotated_in / (eigen_in + damping)
    scaled_out = rotated_out / (eigen_out + damping)
    flat_in = query_in.reshape(QUERIES * RANK, D).astype(jnp.float32)
    flat_out = query_out.reshape(QUERIES * RANK, D).astype(jnp.float32)
    pair_in = jnp.dot(flat_in, scaled_in.T, precision=lax.Precision.HIGHEST, preferred_element_type=jnp.float32)
    pair_out = jnp.dot(flat_out, scaled_out.T, precision=lax.Precision.HIGHEST, preferred_element_type=jnp.float32)
    return (pair_in * pair_out).reshape(QUERIES, RANK, TOKENS).sum(axis=1)
```

```python
import jax
import jax.numpy as jnp
from jax import lax
from jax.experimental import pallas as pl
from jax.experimental.pallas import tpu as pltpu
from jax.sharding import PartitionSpec as P

damping = 0.1
MESH = pl.DeviceIdType.MESH
N_SEM = 160
NT = (((1,), (1,)), ((), ()))


def kernel(total_tokens, li, og, bi, bo, qi, qo, out, X, BAS, A, ACC, AR, S, PS, RF, RN, PR, SC, ss, rs, lx, lb, la):
    acts, bases, queries = (li, og), (bi, bo), (qi, qo)
    w, t, q = lax.axis_index("width"), lax.axis_index("token"), lax.axis_index("query")
    x, z, c = w // 8, lax.rem(w // 2, 4), lax.rem(w, 2)
    xq, cq = 1 - x, 1 - c
    zu, zd, zf = lax.rem(z + 1, 4), lax.rem(z + 3, 4), lax.rem(z + 2, 4)
    tu, td, tf = lax.rem(t + 1, 4), lax.rem(t + 3, 4), lax.rem(t + 2, 4)

    def at(px, pz, pc):
        return (px * 4 + pz) * 2 + pc

    dev_x, dev_c = {"width": at(xq, z, c)}, {"width": at(x, z, cq)}
    dev_u, dev_d = {"width": at(x, zu, c)}, {"width": at(x, zd, c)}
    dev_o = {"width": at(xq, z, c), "query": 1 - q}
    dev_tu, dev_td = {"token": tu}, {"token": td}
    half = X.shape[2] // 2
    rows = X.shape[2]
    upper, lower = pl.ds(0, half), pl.ds(half, half)

    keys, pending = {}, []

    def number(key):
        return keys.setdefault(key, len(keys))

    def send(key, src, dst, dev):
        i = number(key)
        copy = pltpu.make_async_remote_copy(
            src_ref=src, dst_ref=dst, send_sem=ss.at[i], recv_sem=rs.at[i], device_id=dev, device_id_type=MESH
        )
        copy.start()
        pending.append(copy)

    def arrive(key, region, dev=None):
        i = number(key)
        pltpu.make_async_remote_copy(
            src_ref=region, dst_ref=region, send_sem=ss.at[i], recv_sem=rs.at[i],
            device_id=dev_c if dev is None else dev, device_id_type=MESH,
        ).wait_recv()

    me = at(x, z, c)
    own_x = [pltpu.make_async_copy(acts[a], X.at[a, me], lx.at[a]) for a in range(2)]
    for cp in own_x:
        cp.start()
    order = [(x, z), (xq, z), (x, zd), (x, zu), (xq, zd), (xq, zu), (x, zf), (xq, zf)]
    base_copies = {}
    for a in range(2):
        for n, (px, pz) in enumerate(order):
            pair = pl.ds((px * 4 + pz) * 2, 2)
            base_copies[a, n] = pltpu.make_async_copy(bases[a].at[pair], BAS.at[a, pair], lb.at[a, n])
            base_copies[a, n].start()
    src_me = x * 2 + c
    own_a = [pltpu.make_async_copy(queries[a].at[x, :, c], A.at[a, src_me], la.at[a]) for a in range(2)]
    for cp in own_a:
        cp.start()

    barrier = pltpu.get_barrier_semaphore()
    met = 0
    for d in range(1, 16):
        pl.semaphore_signal(barrier, inc=1, device_id={"width": lax.rem(w + d, 16)}, device_id_type=MESH)
        met += 1
    eight = t * 2 + q
    mates = []
    for d in range(1, 8):
        m = lax.rem(eight + d, 8)
        mates.append((m, {"token": m // 2, "query": lax.rem(m, 2)}))
        pl.semaphore_signal(barrier, inc=1, device_id=mates[-1][1], device_id_type=MESH)
        met += 1
    pl.semaphore_signal(barrier, inc=1, device_id=dev_o, device_id_type=MESH)
    met += 1
    pl.semaphore_wait(barrier, met)

    done_pairs = [0, 0]

    def rotate(a, n):
        base_copies[a, n].wait()
        px, pz = order[n]
        first = (px * 4 + pz) * 2
        for col in range(0, 512, 256):
            cols = pl.ds(col, 256)
            part = jnp.dot(X[a, first], BAS[a, first, :, cols], preferred_element_type=jnp.float32)
            part += jnp.dot(X[a, first + 1], BAS[a, first + 1, :, cols], preferred_element_type=jnp.float32)
            if done_pairs[a]:
                part += ACC[a, :, cols]
            ACC[a, :, cols] = part
        done_pairs[a] += 1

    def open_x(a):
        own_x[a].wait()
        send(("x", a), X.at[a, me], X.at[a, me], dev_x)
        send(("c", a), X.at[a, me], X.at[a, me], dev_c)

    def open_z(a):
        send(("zu", a), X.at[a, me], X.at[a, me], dev_u)
        send(("zd", a), X.at[a, me], X.at[a, me], dev_d)

    def from_core(key, a, px, pz):
        arrive(key, X.at[a, at(px, pz, cq)])

    def to_core(key, a, px, pz):
        blk = X.at[a, at(px, pz, c)]
        send(key, blk, blk, dev_c)

    def step1(a):
        blk = X.at[a, at(xq, z, c)]
        arrive(("x", a), blk)
        send(("xzu", a), blk, blk, dev_u)
        send(("xzd", a), blk, blk, dev_d)
        to_core(("cx", a), a, xq, z)
        from_core(("c", a), a, x, z)
        rotate(a, 0)
        from_core(("cx", a), a, xq, z)
        rotate(a, 1)

    def step2(a, px, tag, n):
        up, down = at(px, zd, c), at(px, zu, c)
        arrive((tag + "zu", a), X.at[a, up])
        send((tag + "fu", a), X.at[a, up, upper], X.at[a, up, upper], dev_u)
        to_core((tag + "czu", a), a, px, zd)
        arrive((tag + "zd", a), X.at[a, down])
        send((tag + "fd", a), X.at[a, down, lower], X.at[a, down, lower], dev_d)
        to_core((tag + "czd", a), a, px, zu)
        from_core((tag + "czu", a), a, px, zd)
        rotate(a, n)
        from_core((tag + "czd", a), a, px, zu)
        rotate(a, n + 1)

    def step3(a, px, tag, n):
        far = at(px, zf, c)
        arrive((tag + "fu", a), X.at[a, far, upper])
        arrive((tag + "fd", a), X.at[a, far, lower])
        to_core((tag + "cf", a), a, px, zf)
        from_core((tag + "cf", a), a, px, zf)
        rotate(a, n)

    def squares(a):
        val = ACC[a]
        AR[a, eight] = jnp.sum((val * val).reshape(rows // 8, 8, 512), axis=0)
        for d, (m, dev) in enumerate(mates):
            send(("ar", a, d), AR.at[a, eight], AR.at[a, eight], dev)

    def scale(a):
        for d in range(7):
            arrive(("ar", a, d), AR.at[a, lax.rem(eight + 7 - d, 8)])
        tot = AR[a, 0]
        for k in range(1, 8):
            tot += AR[a, k]
        inv = 1.0 / (jnp.sum(tot, axis=0, keepdims=True) / total_tokens + damping)
        val = ACC[a] * inv
        hi = val.astype(jnp.bfloat16)
        S[a, q, src_me, pl.ds(0, rows)] = hi
        S[a, q, src_me, pl.ds(rows, rows)] = (val - hi.astype(jnp.float32)).astype(jnp.bfloat16)
        blk = S.at[a, q, src_me]
        send(("bx", a), blk, blk, dev_x)
        send(("bo", a), blk, blk, dev_o)
        send(("bc", a), blk, blk, dev_c)

    his, los = pl.ds(0, rows), pl.ds(rows, rows)
    p = 1 - q

    def share(a):
        bx = S.at[a, q, xq * 2 + c]
        arrive(("bx", a), bx)
        hi = S.at[a, q, xq * 2 + c, his]
        send(("bh", a), hi, hi, dev_o)
        send(("bcx", a), bx, bx, dev_c)
        bo_ = S.at[a, p, xq * 2 + c]
        arrive(("bo", a), bo_)
        lo = S.at[a, p, xq * 2 + c, los]
        send(("bl", a), lo, lo, dev_x)
        send(("bco", a), bo_, bo_, dev_c)

    def share_far(a):
        arrive(("bh", a), S.at[a, p, x * 2 + c, his])
        arrive(("bl", a), S.at[a, p, x * 2 + c, los])
        blk = S.at[a, p, x * 2 + c]
        send(("bcf", a), blk, blk, dev_c)

    def own_ready(a):
        arrive(("bc", a), S.at[a, q, x * 2 + cq])
        arrive(("bcx", a), S.at[a, q, xq * 2 + cq])

    def other_ready(a):
        arrive(("bco", a), S.at[a, p, xq * 2 + cq])
        arrive(("bcf", a), S.at[a, p, x * 2 + cq])

    def open_a(a):
        send(("ac", a), queries[a].at[x, :, cq], A.at[a, src_me], dev_c)

    def open_ax(a):
        for k in range(2):
            send_ax(a, k)

    def send_ax(a, k):
        pc = c if k == 0 else cq
        send(("ax", a, k), queries[a].at[xq, t, pc], A.at[a, src_me, t], {"width": at(xq, z, pc)})

    def spread_a(a):
        for k in range(2):
            pc = c if k == 0 else cq
            arrive(("ax", a, k), A.at[a, xq * 2 + pc, t])
        both = pl.ds(xq * 2, 2)
        send(("ayu", a), A.at[a, both, t], A.at[a, both, t], dev_tu)
        send(("ayd", a), A.at[a, both, t], A.at[a, both, t], dev_td)

    def spread_a2(a):
        both = pl.ds(xq * 2, 2)
        arrive(("ayu", a), A.at[a, both, td])
        one = A.at[a, xq * 2, td]
        send(("agu", a), one, one, dev_tu)
        arrive(("ayd", a), A.at[a, both, tu])
        two = A.at[a, xq * 2 + 1, tu]
        send(("agd", a), two, two, dev_td)

    def a_ready(a):
        own_a[a].wait()
        arrive(("ac", a), A.at[a, x * 2 + cq])
        arrive(("agu", a), A.at[a, xq * 2, tf])
        arrive(("agd", a), A.at[a, xq * 2 + 1, tf])

    def pair(a, h, zz):
        hq = q if h == 0 else p
        acc = None
        for k in range(4):
            part = lax.dot_general(S[a, hq, k], A[a, k, zz], NT, preferred_element_type=jnp.float32)
            acc = part if acc is None else acc + part
        PS[a, h, zz] = acc[:rows] + acc[rows:]

    def pairs(a, h):
        pair(a, h, zf)
        send(("pfu", a, h), PS.at[a, h, zf, upper], RF.at[a, h, 0], dev_u)
        send(("pfd", a, h), PS.at[a, h, zf, lower], RF.at[a, h, 1], dev_d)
        pair(a, h, zu)
        pair(a, h, zd)
        arrive(("pfu", a, h), RF.at[a, h, 0])
        PS[a, h, zu, upper] += RF[a, h, 0]
        send(("pnu", a, h), PS.at[a, h, zu], RN.at[a, h, 0], dev_u)
        arrive(("pfd", a, h), RF.at[a, h, 1])
        PS[a, h, zd, lower] += RF[a, h, 1]
        send(("pnd", a, h), PS.at[a, h, zd], RN.at[a, h, 1], dev_d)
        pair(a, h, z)

    def whole(a, h):
        arrive(("pnu", a, h), RN.at[a, h, 0])
        arrive(("pnd", a, h), RN.at[a, h, 1])
        return PS[a, h, z] + RN[a, h, 0] + RN[a, h, 1]

    open_x(0)
    open_z(0)
    open_x(1)
    open_ax(0)
    open_a(0)
    open_a(1)
    step1(0)
    step2(0, x, "", 2)
    step2(0, xq, "x", 4)
    open_z(1)
    step3(0, x, "", 6)
    step3(0, xq, "x", 7)
    squares(0)
    step1(1)
    step2(1, x, "", 2)
    scale(0)
    open_ax(1)
    spread_a(0)
    step2(1, xq, "x", 4)
    step3(1, x, "", 6)
    step3(1, xq, "x", 7)
    squares(1)
    share(0)
    spread_a2(0)
    own_ready(0)
    scale(1)
    share_far(0)
    a_ready(0)
    pairs(0, 0)
    other_ready(0)
    spread_a(1)
    pairs(0, 1)
    share(1)
    spread_a2(1)
    own_ready(1)
    share_far(1)
    a_ready(1)
    pairs(1, 0)
    other_ready(1)
    pairs(1, 1)
    for h in range(2):
        hq = q if h == 0 else p
        PR[pl.ds(hq * rows, rows)] = whole(0, h) * whole(1, h)
    ranks = 32
    pick = (
        lax.broadcasted_iota(jnp.int32, (8, 256), 1) // ranks == lax.broadcasted_iota(jnp.int32, (8, 256), 0)
    ).astype(jnp.float32)
    SC[w] = lax.dot_general(
        pick, PR[...], NT, precision=lax.Precision.HIGHEST, preferred_element_type=jnp.float32
    )
    for d in range(1, 16):
        send(("sc", d), SC.at[w], SC.at[w], {"width": lax.rem(w + d, 16)})
    for d in range(1, 16):
        arrive(("sc", d), SC.at[lax.rem(w + 16 - d, 16)])
    out[...] = SC[...]
    for copy in pending:
        copy.wait_send()
    assert len(keys) <= N_SEM


def on_device(layer_inputs, out_grads, basis_in, basis_out, query_in, query_out):
    total_tokens = layer_inputs.shape[0] * lax.axis_size("token") * lax.axis_size("query")
    rows, cols = layer_inputs.shape
    f32, bf16 = jnp.float32, jnp.bfloat16
    hbm = pl.BlockSpec(memory_space=pl.ANY)
    scores = pl.pallas_call(
        lambda *refs: kernel(total_tokens, *refs),
        out_shape=jax.ShapeDtypeStruct((16, 8, 2 * rows), f32),
        in_specs=[hbm] * 6,
        out_specs=pl.BlockSpec(memory_space=pltpu.VMEM),
        scratch_shapes=[
            pltpu.VMEM((2, 16, rows, cols), bf16),
            pltpu.VMEM((2, 16, cols, cols), bf16),
            pltpu.VMEM((2, 4, 4, 256, cols), bf16),
            pltpu.VMEM((2, rows, cols), f32),
            pltpu.VMEM((2, 8, 8, cols), f32),
            pltpu.VMEM((2, 2, 4, 2 * rows, cols), bf16),
            pltpu.VMEM((2, 2, 4, rows, 256), f32),
            pltpu.VMEM((2, 2, 2, rows // 2, 256), f32),
            pltpu.VMEM((2, 2, 2, rows, 256), f32),
            pltpu.VMEM((2 * rows, 256), f32),
            pltpu.VMEM((16, 8, 2 * rows), f32),
            pltpu.SemaphoreType.DMA((N_SEM,)),
            pltpu.SemaphoreType.DMA((N_SEM,)),
            pltpu.SemaphoreType.DMA((2,)),
            pltpu.SemaphoreType.DMA((2, 8)),
            pltpu.SemaphoreType.DMA((2,)),
        ],
        compiler_params=pltpu.CompilerParams(
            collective_id=0, has_side_effects=True, vmem_limit_bytes=60 * 1024 * 1024
        ),
        name="influence",
    )(
        layer_inputs,
        out_grads,
        basis_in.reshape(16, cols, cols),
        basis_out.reshape(16, cols, cols),
        query_in.reshape(2, 4, 2, 256, cols),
        query_out.reshape(2, 4, 2, 256, cols),
    )
    return scores.reshape(128, 2 * rows)


def solution(mesh):
    return jax.shard_map(
        on_device,
        mesh=mesh,
        in_specs=(
            P(("token", "query"), "width"),
            P(("token", "query"), "width"),
            P(None, "width"),
            P(None, "width"),
            P("query", None, "width"),
            P("query", None, "width"),
        ),
        out_specs=P("query", "token"),
        check_vma=False,
    )
```

```python
import jax
import jax.numpy as jnp
from jax import lax
from jax.experimental import pallas as pl
from jax.experimental.pallas import tpu as pltpu
from jax.sharding import PartitionSpec as P

damping = 0.1
MESH = pl.DeviceIdType.MESH
N_SEM = 160
NT = (((1,), (1,)), ((), ()))


def kernel(total_tokens, li, og, bi, bo, qi, qo, out, X, BAS, A, ACC, AR, S, PS, RF, RN, PR, SC, ss, rs, lx, lb, la):
    acts, bases, queries = (li, og), (bi, bo), (qi, qo)
    w, t, q = lax.axis_index("width"), lax.axis_index("token"), lax.axis_index("query")
    x, z, c = w // 8, lax.rem(w // 2, 4), lax.rem(w, 2)
    xq, cq = 1 - x, 1 - c
    zu, zd, zf = lax.rem(z + 1, 4), lax.rem(z + 3, 4), lax.rem(z + 2, 4)
    tu, td, tf = lax.rem(t + 1, 4), lax.rem(t + 3, 4), lax.rem(t + 2, 4)

    def at(px, pz, pc):
        return (px * 4 + pz) * 2 + pc

    dev_x, dev_c = {"width": at(xq, z, c)}, {"width": at(x, z, cq)}
    dev_u, dev_d = {"width": at(x, zu, c)}, {"width": at(x, zd, c)}
    dev_o = {"width": at(xq, z, c), "query": 1 - q}
    dev_tu, dev_td = {"token": tu}, {"token": td}
    half = X.shape[2] // 2
    rows = X.shape[2]
    upper, lower = pl.ds(0, half), pl.ds(half, half)

    keys, pending, sent, got = {}, [], {}, set()

    def number(key):
        return keys.setdefault(key, len(keys))

    def send(key, src, dst, dev):
        i = number(key)
        copy = pltpu.make_async_remote_copy(
            src_ref=src, dst_ref=dst, send_sem=ss.at[i], recv_sem=rs.at[i], device_id=dev, device_id_type=MESH
        )
        copy.start()
        pending.append(copy)
        sent[key] = dst

    def arrive(key, region, dev=None):
        got.add(key)
        i = number(key)
        pltpu.make_async_remote_copy(
            src_ref=region, dst_ref=region, send_sem=ss.at[i], recv_sem=rs.at[i],
            device_id=dev_c if dev is None else dev, device_id_type=MESH,
        ).wait_recv()

    waited = set()
    me = at(x, z, c)
    own_x = [pltpu.make_async_copy(acts[a], X.at[a, me], lx.at[a]) for a in range(2)]
    for cp in own_x:
        cp.start()
    order = [(x, z), (xq, z), (x, zd), (x, zu), (xq, zd), (xq, zu), (x, zf), (xq, zf)]
    base_copies = {}
    for a in range(2):
        for n, (px, pz) in enumerate(order):
            pair = pl.ds((px * 4 + pz) * 2, 2)
            base_copies[a, n] = pltpu.make_async_copy(bases[a].at[pair], BAS.at[a, pair], lb.at[a, n])
    src_me = x * 2 + c
    own_a = [pltpu.make_async_copy(queries[a].at[x, :, c], A.at[a, src_me], la.at[a]) for a in range(2)]

    def load(a):
        for n in range(8):
            base_copies[a, n].start()

    load(0)
    barrier = pltpu.get_barrier_semaphore()
    met = 0
    for d in range(1, 16):
        pl.semaphore_signal(barrier, inc=1, device_id={"width": lax.rem(w + d, 16)}, device_id_type=MESH)
        met += 1
    eight = t * 2 + q
    mates = []
    for d in range(1, 8):
        m = lax.rem(eight + d, 8)
        mates.append((m, {"token": m // 2, "query": lax.rem(m, 2)}))
        pl.semaphore_signal(barrier, inc=1, device_id=mates[-1][1], device_id_type=MESH)
        met += 1
    pl.semaphore_signal(barrier, inc=1, device_id=dev_o, device_id_type=MESH)
    met += 1
    pl.semaphore_wait(barrier, met)

    done_pairs = [0, 0]

    def rotate(a, n):
        waited.add(id(base_copies[a, n])); base_copies[a, n].wait()
        px, pz = order[n]
        first = (px * 4 + pz) * 2
        for col in range(0, 512, 256):
            cols = pl.ds(col, 256)
            part = jnp.dot(X[a, first], BAS[a, first, :, cols], preferred_element_type=jnp.float32)
            part += jnp.dot(X[a, first + 1], BAS[a, first + 1, :, cols], preferred_element_type=jnp.float32)
            if done_pairs[a]:
                part += ACC[a, :, cols]
            ACC[a, :, cols] = part
        done_pairs[a] += 1

    def open_x(a):
        waited.add(id(own_x[a])); own_x[a].wait()
        send(("x", a), X.at[a, me], X.at[a, me], dev_x)
        send(("c", a), X.at[a, me], X.at[a, me], dev_c)

    def open_z(a):
        send(("zu", a), X.at[a, me], X.at[a, me], dev_u)
        send(("zd", a), X.at[a, me], X.at[a, me], dev_d)

    def from_core(key, a, px, pz):
        arrive(key, X.at[a, at(px, pz, cq)])

    def to_core(key, a, px, pz):
        blk = X.at[a, at(px, pz, c)]
        send(key, blk, blk, dev_c)

    def step1(a):
        blk = X.at[a, at(xq, z, c)]
        arrive(("x", a), blk)
        send(("xzu", a), blk, blk, dev_u)
        send(("xzd", a), blk, blk, dev_d)
        to_core(("cx", a), a, xq, z)
        from_core(("c", a), a, x, z)
        rotate(a, 0)
        from_core(("cx", a), a, xq, z)
        rotate(a, 1)

    def step2(a, px, tag, n):
        up, down = at(px, zd, c), at(px, zu, c)
        arrive((tag + "zu", a), X.at[a, up])
        send((tag + "fu", a), X.at[a, up, upper], X.at[a, up, upper], dev_u)
        to_core((tag + "czu", a), a, px, zd)
        arrive((tag + "zd", a), X.at[a, down])
        send((tag + "fd", a), X.at[a, down, lower], X.at[a, down, lower], dev_d)
        to_core((tag + "czd", a), a, px, zu)
        from_core((tag + "czu", a), a, px, zd)
        rotate(a, n)
        from_core((tag + "czd", a), a, px, zu)
        rotate(a, n + 1)

    def step3(a, px, tag, n):
        far = at(px, zf, c)
        arrive((tag + "fu", a), X.at[a, far, upper])
        arrive((tag + "fd", a), X.at[a, far, lower])
        to_core((tag + "cf", a), a, px, zf)
        from_core((tag + "cf", a), a, px, zf)
        rotate(a, n)

    def squares(a):
        val = ACC[a]
        AR[a, eight] = jnp.sum((val * val).reshape(rows // 8, 8, 512), axis=0)
        for d, (m, dev) in enumerate(mates):
            send(("ar", a, d), AR.at[a, eight], AR.at[a, eight], dev)

    def scale(a):
        for d in range(7):
            arrive(("ar", a, d), AR.at[a, lax.rem(eight + 7 - d, 8)])
        tot = AR[a, 0]
        for k in range(1, 8):
            tot += AR[a, k]
        inv = 1.0 / (jnp.sum(tot, axis=0, keepdims=True) / total_tokens + damping)
        val = ACC[a] * inv
        hi = val.astype(jnp.bfloat16)
        S[a, q, src_me, pl.ds(0, rows)] = hi
        S[a, q, src_me, pl.ds(rows, rows)] = (val - hi.astype(jnp.float32)).astype(jnp.bfloat16)
        blk = S.at[a, q, src_me]
        send(("bx", a), blk, blk, dev_x)
        send(("bo", a), blk, blk, dev_o)
        send(("bc", a), blk, blk, dev_c)

    his, los = pl.ds(0, rows), pl.ds(rows, rows)
    p = 1 - q

    def share(a):
        bx = S.at[a, q, xq * 2 + c]
        arrive(("bx", a), bx)
        hi = S.at[a, q, xq * 2 + c, his]
        send(("bh", a), hi, hi, dev_o)
        send(("bcx", a), bx, bx, dev_c)
        bo_ = S.at[a, p, xq * 2 + c]
        arrive(("bo", a), bo_)
        lo = S.at[a, p, xq * 2 + c, los]
        send(("bl", a), lo, lo, dev_x)
        send(("bco", a), bo_, bo_, dev_c)

    def share_far(a):
        arrive(("bh", a), S.at[a, p, x * 2 + c, his])
        arrive(("bl", a), S.at[a, p, x * 2 + c, los])
        blk = S.at[a, p, x * 2 + c]
        send(("bcf", a), blk, blk, dev_c)

    def own_ready(a):
        arrive(("bc", a), S.at[a, q, x * 2 + cq])
        arrive(("bcx", a), S.at[a, q, xq * 2 + cq])

    def other_ready(a):
        arrive(("bco", a), S.at[a, p, xq * 2 + cq])
        arrive(("bcf", a), S.at[a, p, x * 2 + cq])

    def open_a(a):
        own_a[a].start()
        send(("ac", a), queries[a].at[x, :, cq], A.at[a, src_me], dev_c)

    def ax(a, k):
        pc = c if k == 0 else cq
        send(("ax", a, k), queries[a].at[xq, t, pc], A.at[a, src_me, t], {"width": at(xq, z, pc)})

    def spread(a, k):
        pc = c if k == 0 else cq
        blk = A.at[a, xq * 2 + pc, t]
        arrive(("ax", a, k), blk)
        send(("ayu", a, k), blk, blk, dev_tu)
        send(("ayd", a, k), blk, blk, dev_td)

    def spread2(a):
        blk = A.at[a, xq * 2 + c, td]
        arrive(("ayu", a, 0), blk)
        send(("agu", a), blk, blk, dev_tu)

    def spread3(a):
        blk = A.at[a, xq * 2 + cq, tu]
        arrive(("ayd", a, 1), blk)
        send(("agd", a), blk, blk, dev_td)

    def a_ready(a):
        waited.add(id(own_a[a])); own_a[a].wait()
        arrive(("ac", a), A.at[a, x * 2 + cq])
        arrive(("ayu", a, 1), A.at[a, xq * 2 + cq, td])
        arrive(("ayd", a, 0), A.at[a, xq * 2 + c, tu])
        arrive(("agu", a), A.at[a, xq * 2 + c, tf])
        arrive(("agd", a), A.at[a, xq * 2 + cq, tf])

    def pair(a, h, zz):
        hq = q if h == 0 else p
        acc = None
        for k in range(4):
            part = lax.dot_general(S[a, hq, k], A[a, k, zz], NT, preferred_element_type=jnp.float32)
            acc = part if acc is None else acc + part
        PS[a, h, zz] = acc[:rows] + acc[rows:]

    def pf(a, h):
        pair(a, h, zf)
        send(("pfu", a, h), PS.at[a, h, zf, upper], RF.at[a, h, 0], dev_u)
        send(("pfd", a, h), PS.at[a, h, zf, lower], RF.at[a, h, 1], dev_d)
        pair(a, h, zu)
        send(("pnu", a, h, 0), PS.at[a, h, zu, lower], RN.at[a, h, 0, lower], dev_u)
        pair(a, h, zd)
        send(("pnd", a, h, 0), PS.at[a, h, zd, upper], RN.at[a, h, 1, upper], dev_d)
        pair(a, h, z)

    def pn(a, h):
        arrive(("pfu", a, h), RF.at[a, h, 0])
        PS[a, h, zu, upper] += RF[a, h, 0]
        send(("pnu", a, h, 1), PS.at[a, h, zu, upper], RN.at[a, h, 0, upper], dev_u)
        arrive(("pfd", a, h), RF.at[a, h, 1])
        PS[a, h, zd, lower] += RF[a, h, 1]
        send(("pnd", a, h, 1), PS.at[a, h, zd, lower], RN.at[a, h, 1, lower], dev_d)

    def whole(a, h):
        for n, part in enumerate((lower, upper)):
            arrive(("pnu", a, h, n), RN.at[a, h, 0, part])
        for n, part in enumerate((upper, lower)):
            arrive(("pnd", a, h, n), RN.at[a, h, 1, part])
        return PS[a, h, z] + RN[a, h, 0] + RN[a, h, 1]

    open_x(0)
    open_z(0)
    open_x(1)
    ax(0, 0)
    ax(0, 1)
    ax(1, 0)
    step1(0)
    load(1)
    step2(0, x, "", 2)
    step2(0, xq, "x", 4)
    open_z(1)
    step3(0, x, "", 6)
    step3(0, xq, "x", 7)
    squares(0)
    step1(1)
    open_a(0)
    spread(0, 0)
    step2(1, x, "", 2)
    scale(0)
    ax(1, 1)
    spread(0, 1)
    step2(1, xq, "x", 4)
    spread2(0)
    step3(1, x, "", 6)
    step3(1, xq, "x", 7)
    squares(1)
    spread3(0)
    open_a(1)
    spread(1, 0)
    share(0)
    scale(1)
    own_ready(0)
    a_ready(0)
    pf(0, 0)
    pn(0, 0)
    spread(1, 1)
    share_far(0)
    other_ready(0)
    pf(0, 1)
    spread2(1)
    pn(0, 1)
    spread3(1)
    share(1)
    own_ready(1)
    a_ready(1)
    pf(1, 0)
    pn(1, 0)
    share_far(1)
    other_ready(1)
    pf(1, 1)
    pn(1, 1)
    for h in range(2):
        hq = q if h == 0 else p
        PR[pl.ds(hq * rows, rows)] = whole(0, h) * whole(1, h)
    ranks = 32
    pick = (
        lax.broadcasted_iota(jnp.int32, (8, 256), 1) // ranks == lax.broadcasted_iota(jnp.int32, (8, 256), 0)
    ).astype(jnp.float32)
    SC[w] = lax.dot_general(
        pick, PR[...], NT, precision=lax.Precision.HIGHEST, preferred_element_type=jnp.float32
    )
    for d in range(1, 16):
        send(("sc", d), SC.at[w], SC.at[w], {"width": lax.rem(w + d, 16)})
    for d in range(1, 16):
        arrive(("sc", d), SC.at[lax.rem(w + 16 - d, 16)])
    out[...] = SC[...]
    for copy in pending:
        copy.wait_send()
    assert len(keys) <= N_SEM


def on_device(layer_inputs, out_grads, basis_in, basis_out, query_in, query_out):
    total_tokens = layer_inputs.shape[0] * lax.axis_size("token") * lax.axis_size("query")
    rows, cols = layer_inputs.shape
    f32, bf16 = jnp.float32, jnp.bfloat16
    hbm = pl.BlockSpec(memory_space=pl.ANY)
    scores = pl.pallas_call(
        lambda *refs: kernel(total_tokens, *refs),
        out_shape=jax.ShapeDtypeStruct((16, 8, 2 * rows), f32),
        in_specs=[hbm] * 6,
        out_specs=pl.BlockSpec(memory_space=pltpu.VMEM),
        scratch_shapes=[
            pltpu.VMEM((2, 16, rows, cols), bf16),
            pltpu.VMEM((2, 16, cols, cols), bf16),
            pltpu.VMEM((2, 4, 4, 256, cols), bf16),
            pltpu.VMEM((2, rows, cols), f32),
            pltpu.VMEM((2, 8, 8, cols), f32),
            pltpu.VMEM((2, 2, 4, 2 * rows, cols), bf16),
            pltpu.VMEM((2, 2, 4, rows, 256), f32),
            pltpu.VMEM((2, 2, 2, rows // 2, 256), f32),
            pltpu.VMEM((2, 2, 2, rows, 256), f32),
            pltpu.VMEM((2 * rows, 256), f32),
            pltpu.VMEM((16, 8, 2 * rows), f32),
            pltpu.SemaphoreType.DMA((N_SEM,)),
            pltpu.SemaphoreType.DMA((N_SEM,)),
            pltpu.SemaphoreType.DMA((2,)),
            pltpu.SemaphoreType.DMA((2, 8)),
            pltpu.SemaphoreType.DMA((2,)),
        ],
        compiler_params=pltpu.CompilerParams(
            collective_id=0, has_side_effects=True, vmem_limit_bytes=60 * 1024 * 1024
        ),
        name="influence",
    )(
        layer_inputs,
        out_grads,
        basis_in.reshape(16, cols, cols),
        basis_out.reshape(16, cols, cols),
        query_in.reshape(2, 4, 2, 256, cols),
        query_out.reshape(2, 4, 2, 256, cols),
    )
    return scores.reshape(128, 2 * rows)


def solution(mesh):
    return jax.shard_map(
        on_device,
        mesh=mesh,
        in_specs=(
            P(("token", "query"), "width"),
            P(("token", "query"), "width"),
            P(None, "width"),
            P(None, "width"),
            P("query", None, "width"),
            P("query", None, "width"),
        ),
        out_specs=P("query", "token"),
        check_vma=False,
    )
```

```python
import jax
import jax.numpy as jnp
from jax import lax
from jax.experimental import pallas as pl
from jax.experimental.pallas import tpu as pltpu
from jax.sharding import PartitionSpec as P

damping = 0.1
MESH = pl.DeviceIdType.MESH
N_SEM = 160
SPLIT = (False, True)
NT = (((1,), (1,)), ((), ()))


def kernel(total_tokens, li, og, bi, bo, qi, qo, out, X, BAS, A, ACC, AR, S, PS, RF, RN, PR, SC, ss, rs, lx, lb, la):
    acts, bases, queries = (li, og), (bi, bo), (qi, qo)
    w, t, q = lax.axis_index("width"), lax.axis_index("token"), lax.axis_index("query")
    x, z, c = w // 8, lax.rem(w // 2, 4), lax.rem(w, 2)
    xq, cq = 1 - x, 1 - c
    zu, zd, zf = lax.rem(z + 1, 4), lax.rem(z + 3, 4), lax.rem(z + 2, 4)
    tu, td, tf = lax.rem(t + 1, 4), lax.rem(t + 3, 4), lax.rem(t + 2, 4)

    def at(px, pz, pc):
        return (px * 4 + pz) * 2 + pc

    dev_x, dev_c = {"width": at(xq, z, c)}, {"width": at(x, z, cq)}
    dev_u, dev_d = {"width": at(x, zu, c)}, {"width": at(x, zd, c)}
    dev_o = {"width": at(xq, z, c), "query": 1 - q}
    dev_tu, dev_td = {"token": tu}, {"token": td}
    half = X.shape[2] // 2
    rows = X.shape[2]
    upper, lower = pl.ds(0, half), pl.ds(half, half)

    keys, pending, sent, got = {}, [], {}, set()

    def number(key):
        return keys.setdefault(key, len(keys))

    def send(key, src, dst, dev):
        i = number(key)
        copy = pltpu.make_async_remote_copy(
            src_ref=src, dst_ref=dst, send_sem=ss.at[i], recv_sem=rs.at[i], device_id=dev, device_id_type=MESH
        )
        copy.start()
        pending.append(copy)
        sent[key] = dst

    def arrive(key, region, dev=None):
        got.add(key)
        i = number(key)
        pltpu.make_async_remote_copy(
            src_ref=region, dst_ref=region, send_sem=ss.at[i], recv_sem=rs.at[i],
            device_id=dev_c if dev is None else dev, device_id_type=MESH,
        ).wait_recv()

    waited = set()
    me = at(x, z, c)
    own_x = [pltpu.make_async_copy(acts[a], X.at[a, me], lx.at[a]) for a in range(2)]
    for cp in own_x:
        cp.start()
    order = [(x, z), (xq, z), (x, zd), (x, zu), (xq, zd), (xq, zu), (x, zf), (xq, zf)]
    base_copies = {}
    for a in range(2):
        for n, (px, pz) in enumerate(order):
            pair = pl.ds((px * 4 + pz) * 2, 2)
            base_copies[a, n] = pltpu.make_async_copy(bases[a].at[pair], BAS.at[a, pair], lb.at[a, n])
    src_me = x * 2 + c
    own_a = [pltpu.make_async_copy(queries[a].at[x, :, c], A.at[a, src_me], la.at[a]) for a in range(2)]

    def load(a):
        for n in range(8):
            base_copies[a, n].start()

    load(0)
    barrier = pltpu.get_barrier_semaphore()
    met = 0
    for d in range(1, 16):
        pl.semaphore_signal(barrier, inc=1, device_id={"width": lax.rem(w + d, 16)}, device_id_type=MESH)
        met += 1
    eight = t * 2 + q
    mates = []
    for d in range(1, 8):
        m = lax.rem(eight + d, 8)
        mates.append((m, {"token": m // 2, "query": lax.rem(m, 2)}))
        pl.semaphore_signal(barrier, inc=1, device_id=mates[-1][1], device_id_type=MESH)
        met += 1
    pl.semaphore_signal(barrier, inc=1, device_id=dev_o, device_id_type=MESH)
    met += 1
    pl.semaphore_wait(barrier, met)

    done_pairs = [0, 0]

    def rotate(a, n):
        waited.add(id(base_copies[a, n])); base_copies[a, n].wait()
        px, pz = order[n]
        first = (px * 4 + pz) * 2
        for col in range(0, 512, 256):
            cols = pl.ds(col, 256)
            part = jnp.dot(X[a, first], BAS[a, first, :, cols], preferred_element_type=jnp.float32)
            part += jnp.dot(X[a, first + 1], BAS[a, first + 1, :, cols], preferred_element_type=jnp.float32)
            if done_pairs[a]:
                part += ACC[a, :, cols]
            ACC[a, :, cols] = part
        done_pairs[a] += 1

    def open_x(a):
        waited.add(id(own_x[a])); own_x[a].wait()
        send(("x", a), X.at[a, me], X.at[a, me], dev_x)
        send(("c", a), X.at[a, me], X.at[a, me], dev_c)

    def open_z(a):
        send(("zu", a), X.at[a, me], X.at[a, me], dev_u)
        send(("zd", a), X.at[a, me], X.at[a, me], dev_d)

    def from_core(key, a, px, pz):
        arrive(key, X.at[a, at(px, pz, cq)])

    def to_core(key, a, px, pz):
        blk = X.at[a, at(px, pz, c)]
        send(key, blk, blk, dev_c)

    def s1(a):
        blk = X.at[a, at(xq, z, c)]
        arrive(("x", a), blk)
        send(("xzu", a), blk, blk, dev_u)
        send(("xzd", a), blk, blk, dev_d)
        to_core(("cx", a), a, xq, z)

    def r1(a):
        from_core(("c", a), a, x, z)
        rotate(a, 0)
        from_core(("cx", a), a, xq, z)
        rotate(a, 1)

    def s2(a, tag):
        px = xq if tag else x
        up, down = at(px, zd, c), at(px, zu, c)
        arrive((tag + "zu", a), X.at[a, up])
        send((tag + "fu", a), X.at[a, up, upper], X.at[a, up, upper], dev_u)
        to_core((tag + "czu", a), a, px, zd)
        arrive((tag + "zd", a), X.at[a, down])
        send((tag + "fd", a), X.at[a, down, lower], X.at[a, down, lower], dev_d)
        to_core((tag + "czd", a), a, px, zu)

    def r2(a, tag):
        px, n = (xq, 4) if tag else (x, 2)
        from_core((tag + "czu", a), a, px, zd)
        rotate(a, n)
        from_core((tag + "czd", a), a, px, zu)
        rotate(a, n + 1)

    def s3(a, tag):
        px = xq if tag else x
        far = at(px, zf, c)
        arrive((tag + "fu", a), X.at[a, far, upper])
        arrive((tag + "fd", a), X.at[a, far, lower])
        to_core((tag + "cf", a), a, px, zf)

    def r3(a, tag):
        px, n = (xq, 7) if tag else (x, 6)
        from_core((tag + "cf", a), a, px, zf)
        rotate(a, n)

    def squares(a):
        val = ACC[a]
        AR[a, eight] = jnp.sum((val * val).reshape(rows // 8, 8, 512), axis=0)
        for d, (m, dev) in enumerate(mates):
            send(("ar", a, d), AR.at[a, eight], AR.at[a, eight], dev)

    def scale(a):
        for d in range(7):
            arrive(("ar", a, d), AR.at[a, lax.rem(eight + 7 - d, 8)])
        tot = AR[a, 0]
        for k in range(1, 8):
            tot += AR[a, k]
        inv = 1.0 / (jnp.sum(tot, axis=0, keepdims=True) / total_tokens + damping)
        val = ACC[a] * inv
        hi = val.astype(jnp.bfloat16)
        S[a, q, src_me, pl.ds(0, rows)] = hi
        S[a, q, src_me, pl.ds(rows, rows)] = (val - hi.astype(jnp.float32)).astype(jnp.bfloat16)
        blk = S.at[a, q, src_me]
        send(("bx", a), blk, blk, dev_x)
        send(("bo", a), blk, blk, dev_o)
        send(("bc", a), blk, blk, dev_c)

    p = 1 - q

    his, los = pl.ds(0, rows), pl.ds(rows, rows)

    def shx(a):
        blk = S.at[a, q, xq * 2 + c]
        arrive(("bx", a), blk)
        part = blk if not SPLIT[a] else S.at[a, q, xq * 2 + c, his]
        send(("bh", a), part, part, dev_o)
        send(("bcx", a), blk, blk, dev_c)

    def sho(a):
        blk = S.at[a, p, xq * 2 + c]
        arrive(("bo", a), blk)
        if SPLIT[a]:
            part = S.at[a, p, xq * 2 + c, los]
            send(("bl", a), part, part, dev_x)
        send(("bco", a), blk, blk, dev_c)

    def sfar(a):
        blk = S.at[a, p, x * 2 + c]
        if SPLIT[a]:
            arrive(("bh", a), S.at[a, p, x * 2 + c, his])
            arrive(("bl", a), S.at[a, p, x * 2 + c, los])
        else:
            arrive(("bh", a), blk)
        send(("bcf", a), blk, blk, dev_c)

    def own_ready(a):
        arrive(("bc", a), S.at[a, q, x * 2 + cq])
        arrive(("bcx", a), S.at[a, q, xq * 2 + cq])

    def other_ready(a):
        arrive(("bco", a), S.at[a, p, xq * 2 + cq])
        arrive(("bcf", a), S.at[a, p, x * 2 + cq])

    def open_a(a):
        own_a[a].start()
        send(("ac", a), queries[a].at[x, :, cq], A.at[a, src_me], dev_c)

    def ax(a, k):
        pc = c if k == 0 else cq
        send(("ax", a, k), queries[a].at[xq, t, pc], A.at[a, src_me, t], {"width": at(xq, z, pc)})

    def spread(a, k):
        pc = c if k == 0 else cq
        blk = A.at[a, xq * 2 + pc, t]
        arrive(("ax", a, k), blk)
        send(("ayu", a, k), blk, blk, dev_tu)
        send(("ayd", a, k), blk, blk, dev_td)

    def spread2(a):
        blk = A.at[a, xq * 2 + c, td]
        arrive(("ayu", a, 0), blk)
        send(("agu", a), blk, blk, dev_tu)

    def spread3(a):
        blk = A.at[a, xq * 2 + cq, tu]
        arrive(("ayd", a, 1), blk)
        send(("agd", a), blk, blk, dev_td)

    def a_ready(a):
        waited.add(id(own_a[a])); own_a[a].wait()
        arrive(("ac", a), A.at[a, x * 2 + cq])
        arrive(("ayu", a, 1), A.at[a, xq * 2 + cq, td])
        arrive(("ayd", a, 0), A.at[a, xq * 2 + c, tu])
        arrive(("agu", a), A.at[a, xq * 2 + c, tf])
        arrive(("agd", a), A.at[a, xq * 2 + cq, tf])

    def pair(a, h, zz):
        hq = q if h == 0 else p
        acc = None
        for k in range(4):
            part = lax.dot_general(S[a, hq, k], A[a, k, zz], NT, preferred_element_type=jnp.float32)
            acc = part if acc is None else acc + part
        PS[a, h, zz] = acc[:rows] + acc[rows:]

    def pf(a, h):
        pair(a, h, zf)
        send(("pfu", a, h), PS.at[a, h, zf, upper], RF.at[a, h, 0], dev_u)
        send(("pfd", a, h), PS.at[a, h, zf, lower], RF.at[a, h, 1], dev_d)
        pair(a, h, zu)
        send(("pnu", a, h, 0), PS.at[a, h, zu, lower], RN.at[a, h, 0, lower], dev_u)
        pair(a, h, zd)
        send(("pnd", a, h, 0), PS.at[a, h, zd, upper], RN.at[a, h, 1, upper], dev_d)
        pair(a, h, z)

    def pn(a, h):
        arrive(("pfu", a, h), RF.at[a, h, 0])
        PS[a, h, zu, upper] += RF[a, h, 0]
        send(("pnu", a, h, 1), PS.at[a, h, zu, upper], RN.at[a, h, 0, upper], dev_u)
        arrive(("pfd", a, h), RF.at[a, h, 1])
        PS[a, h, zd, lower] += RF[a, h, 1]
        send(("pnd", a, h, 1), PS.at[a, h, zd, lower], RN.at[a, h, 1, lower], dev_d)

    def whole(a, h):
        for n, part in enumerate((lower, upper)):
            arrive(("pnu", a, h, n), RN.at[a, h, 0, part])
        for n, part in enumerate((upper, lower)):
            arrive(("pnd", a, h, n), RN.at[a, h, 1, part])
        return PS[a, h, z] + RN[a, h, 0] + RN[a, h, 1]

    open_x(0)
    open_a(1)
    open_x(1)
    load(1)
    ax(0, 0)
    ax(1, 1)
    open_z(0)
    s1(0)
    s2(0, "")
    s2(0, "x")
    s3(0, "")
    spread(0, 0)
    open_z(1)
    r1(0)
    r3(0, "")
    s3(0, "x")
    r2(0, "x")
    r2(0, "")
    r3(0, "x")
    squares(0)
    ax(0, 1)
    s1(1)
    spread(1, 1)
    spread2(0)
    s2(1, "")
    scale(0)
    s2(1, "x")
    open_a(0)
    r1(1)
    spread(0, 1)
    r2(1, "")
    ax(1, 0)
    s3(1, "")
    r2(1, "x")
    r3(1, "")
    s3(1, "x")
    r3(1, "x")
    squares(1)
    spread3(0)
    sho(0)
    shx(0)
    spread(1, 0)
    scale(1)
    own_ready(0)
    a_ready(0)
    pf(0, 0)
    spread3(1)
    sfar(0)
    pn(0, 0)
    other_ready(0)
    spread2(1)
    pf(0, 1)
    shx(1)
    sho(1)
    own_ready(1)
    pn(0, 1)
    a_ready(1)
    pf(1, 0)
    sfar(1)
    pn(1, 0)
    other_ready(1)
    pf(1, 1)
    pn(1, 1)
    for h in range(2):
        hq = q if h == 0 else p
        PR[pl.ds(hq * rows, rows)] = whole(0, h) * whole(1, h)
    ranks = 32
    pick = (
        lax.broadcasted_iota(jnp.int32, (8, 256), 1) // ranks == lax.broadcasted_iota(jnp.int32, (8, 256), 0)
    ).astype(jnp.float32)
    SC[w] = lax.dot_general(
        pick, PR[...], NT, precision=lax.Precision.HIGHEST, preferred_element_type=jnp.float32
    )
    for d in range(1, 16):
        send(("sc", d), SC.at[w], SC.at[w], {"width": lax.rem(w + d, 16)})
    for d in range(1, 16):
        arrive(("sc", d), SC.at[lax.rem(w + 16 - d, 16)])
    out[...] = SC[...]
    for copy in pending:
        copy.wait_send()
    assert len(keys) <= N_SEM


def on_device(layer_inputs, out_grads, basis_in, basis_out, query_in, query_out):
    total_tokens = layer_inputs.shape[0] * lax.axis_size("token") * lax.axis_size("query")
    rows, cols = layer_inputs.shape
    f32, bf16 = jnp.float32, jnp.bfloat16
    hbm = pl.BlockSpec(memory_space=pl.ANY)
    scores = pl.pallas_call(
        lambda *refs: kernel(total_tokens, *refs),
        out_shape=jax.ShapeDtypeStruct((16, 8, 2 * rows), f32),
        in_specs=[hbm] * 6,
        out_specs=pl.BlockSpec(memory_space=pltpu.VMEM),
        scratch_shapes=[
            pltpu.VMEM((2, 16, rows, cols), bf16),
            pltpu.VMEM((2, 16, cols, cols), bf16),
            pltpu.VMEM((2, 4, 4, 256, cols), bf16),
            pltpu.VMEM((2, rows, cols), f32),
            pltpu.VMEM((2, 8, 8, cols), f32),
            pltpu.VMEM((2, 2, 4, 2 * rows, cols), bf16),
            pltpu.VMEM((2, 2, 4, rows, 256), f32),
            pltpu.VMEM((2, 2, 2, rows // 2, 256), f32),
            pltpu.VMEM((2, 2, 2, rows, 256), f32),
            pltpu.VMEM((2 * rows, 256), f32),
            pltpu.VMEM((16, 8, 2 * rows), f32),
            pltpu.SemaphoreType.DMA((N_SEM,)),
            pltpu.SemaphoreType.DMA((N_SEM,)),
            pltpu.SemaphoreType.DMA((2,)),
            pltpu.SemaphoreType.DMA((2, 8)),
            pltpu.SemaphoreType.DMA((2,)),
        ],
        compiler_params=pltpu.CompilerParams(
            collective_id=0, has_side_effects=True, vmem_limit_bytes=60 * 1024 * 1024
        ),
        name="influence",
    )(
        layer_inputs,
        out_grads,
        basis_in.reshape(16, cols, cols),
        basis_out.reshape(16, cols, cols),
        query_in.reshape(2, 4, 2, 256, cols),
        query_out.reshape(2, 4, 2, 256, cols),
    )
    return scores.reshape(128, 2 * rows)


def solution(mesh):
    return jax.shard_map(
        on_device,
        mesh=mesh,
        in_specs=(
            P(("token", "query"), "width"),
            P(("token", "query"), "width"),
            P(None, "width"),
            P(None, "width"),
            P("query", None, "width"),
            P("query", None, "width"),
        ),
        out_specs=P("query", "token"),
        check_vma=False,
    )
```

```python
import jax
import jax.numpy as jnp
from jax import lax
from jax.experimental import pallas as pl
from jax.experimental.pallas import tpu as pltpu
from jax.sharding import PartitionSpec as P

damping = 0.1
MESH = pl.DeviceIdType.MESH
N_SEM = 160
SPLIT = (False, True)
NT = (((1,), (1,)), ((), ()))


def kernel(total_tokens, li, og, bi, bo, qi, qo, out, X, BAS, A, ACC, AR, S, PS, RF, RN, PR, SC, ss, rs, lx, lb, la):
    acts, bases, queries = (li, og), (bi, bo), (qi, qo)
    w, t, q = lax.axis_index("width"), lax.axis_index("token"), lax.axis_index("query")
    x, z, c = w // 8, lax.rem(w // 2, 4), lax.rem(w, 2)
    xq, cq = 1 - x, 1 - c
    zu, zd, zf = lax.rem(z + 1, 4), lax.rem(z + 3, 4), lax.rem(z + 2, 4)
    tu, td, tf = lax.rem(t + 1, 4), lax.rem(t + 3, 4), lax.rem(t + 2, 4)

    def at(px, pz, pc):
        return (px * 4 + pz) * 2 + pc

    dev_x, dev_c = {"width": at(xq, z, c)}, {"width": at(x, z, cq)}
    dev_u, dev_d = {"width": at(x, zu, c)}, {"width": at(x, zd, c)}
    dev_o = {"width": at(xq, z, c), "query": 1 - q}
    dev_tu, dev_td = {"token": tu}, {"token": td}
    half = X.shape[2] // 2
    rows = X.shape[2]
    upper, lower = pl.ds(0, half), pl.ds(half, half)

    keys, pending = {}, []

    def number(key):
        return keys.setdefault(key, len(keys))

    def send(key, src, dst, dev):
        i = number(key)
        copy = pltpu.make_async_remote_copy(
            src_ref=src, dst_ref=dst, send_sem=ss.at[i], recv_sem=rs.at[i], device_id=dev, device_id_type=MESH
        )
        copy.start()
        pending.append(copy)

    def arrive(key, region, dev=None):
        i = number(key)
        pltpu.make_async_remote_copy(
            src_ref=region, dst_ref=region, send_sem=ss.at[i], recv_sem=rs.at[i],
            device_id=dev_c if dev is None else dev, device_id_type=MESH,
        ).wait_recv()

    me = at(x, z, c)
    own_x = [pltpu.make_async_copy(acts[a], X.at[a, me], lx.at[a]) for a in range(2)]
    for cp in own_x:
        cp.start()
    order = [(x, z), (xq, z), (x, zd), (x, zu), (xq, zd), (xq, zu), (x, zf), (xq, zf)]
    base_copies = {}
    for a in range(2):
        for n, (px, pz) in enumerate(order):
            pair = pl.ds((px * 4 + pz) * 2, 2)
            base_copies[a, n] = pltpu.make_async_copy(bases[a].at[pair], BAS.at[a, pair], lb.at[a, n])
    src_me = x * 2 + c
    own_a = [pltpu.make_async_copy(queries[a].at[x, :, c], A.at[a, src_me], la.at[a]) for a in range(2)]

    def load(a):
        for n in range(8):
            base_copies[a, n].start()

    load(0)
    barrier = pltpu.get_barrier_semaphore()
    met = 0
    for d in range(1, 16):
        pl.semaphore_signal(barrier, inc=1, device_id={"width": lax.rem(w + d, 16)}, device_id_type=MESH)
        met += 1
    eight = t * 2 + q
    mates = []
    for d in range(1, 8):
        m = lax.rem(eight + d, 8)
        mates.append((m, {"token": m // 2, "query": lax.rem(m, 2)}))
        pl.semaphore_signal(barrier, inc=1, device_id=mates[-1][1], device_id_type=MESH)
        met += 1
    pl.semaphore_signal(barrier, inc=1, device_id=dev_o, device_id_type=MESH)
    met += 1
    pl.semaphore_wait(barrier, met)

    done_pairs = [0, 0]

    def rotate(a, n):
        base_copies[a, n].wait()
        px, pz = order[n]
        first = (px * 4 + pz) * 2
        for col in range(0, 512, 256):
            cols = pl.ds(col, 256)
            part = jnp.dot(X[a, first], BAS[a, first, :, cols], preferred_element_type=jnp.float32)
            part += jnp.dot(X[a, first + 1], BAS[a, first + 1, :, cols], preferred_element_type=jnp.float32)
            if done_pairs[a]:
                part += ACC[a, :, cols]
            ACC[a, :, cols] = part
        done_pairs[a] += 1

    def open_x(a):
        own_x[a].wait()
        send(("x", a), X.at[a, me], X.at[a, me], dev_x)
        send(("c", a), X.at[a, me], X.at[a, me], dev_c)

    def open_z(a):
        send(("zu", a), X.at[a, me], X.at[a, me], dev_u)
        send(("zd", a), X.at[a, me], X.at[a, me], dev_d)

    def from_core(key, a, px, pz):
        arrive(key, X.at[a, at(px, pz, cq)])

    def to_core(key, a, px, pz):
        blk = X.at[a, at(px, pz, c)]
        send(key, blk, blk, dev_c)

    def s1(a):
        blk = X.at[a, at(xq, z, c)]
        arrive(("x", a), blk)
        send(("xzu", a), blk, blk, dev_u)
        send(("xzd", a), blk, blk, dev_d)
        to_core(("cx", a), a, xq, z)

    def r1(a):
        from_core(("c", a), a, x, z)
        rotate(a, 0)
        from_core(("cx", a), a, xq, z)
        rotate(a, 1)

    def s2(a, tag):
        px = xq if tag else x
        up, down = at(px, zd, c), at(px, zu, c)
        arrive((tag + "zu", a), X.at[a, up])
        send((tag + "fu", a), X.at[a, up, upper], X.at[a, up, upper], dev_u)
        to_core((tag + "czu", a), a, px, zd)
        arrive((tag + "zd", a), X.at[a, down])
        send((tag + "fd", a), X.at[a, down, lower], X.at[a, down, lower], dev_d)
        to_core((tag + "czd", a), a, px, zu)

    def r2(a, tag):
        px, n = (xq, 4) if tag else (x, 2)
        from_core((tag + "czu", a), a, px, zd)
        rotate(a, n)
        from_core((tag + "czd", a), a, px, zu)
        rotate(a, n + 1)

    def s3(a, tag):
        px = xq if tag else x
        far = at(px, zf, c)
        arrive((tag + "fu", a), X.at[a, far, upper])
        arrive((tag + "fd", a), X.at[a, far, lower])
        to_core((tag + "cf", a), a, px, zf)

    def r3(a, tag):
        px, n = (xq, 7) if tag else (x, 6)
        from_core((tag + "cf", a), a, px, zf)
        rotate(a, n)

    def squares(a):
        val = ACC[a]
        AR[a, eight] = jnp.sum((val * val).reshape(rows // 8, 8, 512), axis=0)
        for d, (m, dev) in enumerate(mates):
            send(("ar", a, d), AR.at[a, eight], AR.at[a, eight], dev)

    def scale(a):
        for d in range(7):
            arrive(("ar", a, d), AR.at[a, lax.rem(eight + 7 - d, 8)])
        tot = AR[a, 0]
        for k in range(1, 8):
            tot += AR[a, k]
        inv = 1.0 / (jnp.sum(tot, axis=0, keepdims=True) / total_tokens + damping)
        val = ACC[a] * inv
        hi = val.astype(jnp.bfloat16)
        S[a, q, src_me, pl.ds(0, rows)] = hi
        S[a, q, src_me, pl.ds(rows, rows)] = (val - hi.astype(jnp.float32)).astype(jnp.bfloat16)
        blk = S.at[a, q, src_me]
        send(("bx", a), blk, blk, dev_x)
        send(("bo", a), blk, blk, dev_o)
        send(("bc", a), blk, blk, dev_c)

    p = 1 - q

    his, los = pl.ds(0, rows), pl.ds(rows, rows)

    def shx(a):
        blk = S.at[a, q, xq * 2 + c]
        arrive(("bx", a), blk)
        part = blk if not SPLIT[a] else S.at[a, q, xq * 2 + c, his]
        send(("bh", a), part, part, dev_o)
        send(("bcx", a), blk, blk, dev_c)

    def sho(a):
        blk = S.at[a, p, xq * 2 + c]
        arrive(("bo", a), blk)
        if SPLIT[a]:
            part = S.at[a, p, xq * 2 + c, los]
            send(("bl", a), part, part, dev_x)
        send(("bco", a), blk, blk, dev_c)

    def sfar(a):
        blk = S.at[a, p, x * 2 + c]
        if SPLIT[a]:
            arrive(("bh", a), S.at[a, p, x * 2 + c, his])
            arrive(("bl", a), S.at[a, p, x * 2 + c, los])
        else:
            arrive(("bh", a), blk)
        send(("bcf", a), blk, blk, dev_c)

    def own_ready(a):
        arrive(("bc", a), S.at[a, q, x * 2 + cq])
        arrive(("bcx", a), S.at[a, q, xq * 2 + cq])

    def other_ready(a):
        arrive(("bco", a), S.at[a, p, xq * 2 + cq])
        arrive(("bcf", a), S.at[a, p, x * 2 + cq])

    def open_a(a):
        own_a[a].start()
        send(("ac", a), queries[a].at[x, :, cq], A.at[a, src_me], dev_c)

    def ax(a, k):
        pc = c if k == 0 else cq
        send(("ax", a, k), queries[a].at[xq, t, pc], A.at[a, src_me, t], {"width": at(xq, z, pc)})

    def spread(a, k):
        pc = c if k == 0 else cq
        blk = A.at[a, xq * 2 + pc, t]
        arrive(("ax", a, k), blk)
        send(("ayu", a, k), blk, blk, dev_tu)
        send(("ayd", a, k), blk, blk, dev_td)

    def spread2(a):
        blk = A.at[a, xq * 2 + c, td]
        arrive(("ayu", a, 0), blk)
        send(("agu", a), blk, blk, dev_tu)

    def spread3(a):
        blk = A.at[a, xq * 2 + cq, tu]
        arrive(("ayd", a, 1), blk)
        send(("agd", a), blk, blk, dev_td)

    def a_ready(a):
        own_a[a].wait()
        arrive(("ac", a), A.at[a, x * 2 + cq])
        arrive(("ayu", a, 1), A.at[a, xq * 2 + cq, td])
        arrive(("ayd", a, 0), A.at[a, xq * 2 + c, tu])
        arrive(("agu", a), A.at[a, xq * 2 + c, tf])
        arrive(("agd", a), A.at[a, xq * 2 + cq, tf])

    def pair(a, h, zz):
        hq = q if h == 0 else p
        acc = None
        for k in range(4):
            part = lax.dot_general(S[a, hq, k], A[a, k, zz], NT, preferred_element_type=jnp.float32)
            acc = part if acc is None else acc + part
        PS[a, h, zz] = acc[:rows] + acc[rows:]

    def pf(a, h):
        pair(a, h, zf)
        send(("pfu", a, h), PS.at[a, h, zf, upper], RF.at[a, h, 0], dev_u)
        send(("pfd", a, h), PS.at[a, h, zf, lower], RF.at[a, h, 1], dev_d)
        pair(a, h, zu)
        send(("pnu", a, h, 0), PS.at[a, h, zu, lower], RN.at[a, h, 0, lower], dev_u)
        pair(a, h, zd)
        send(("pnd", a, h, 0), PS.at[a, h, zd, upper], RN.at[a, h, 1, upper], dev_d)
        pair(a, h, z)

    def pn(a, h):
        arrive(("pfu", a, h), RF.at[a, h, 0])
        PS[a, h, zu, upper] += RF[a, h, 0]
        send(("pnu", a, h, 1), PS.at[a, h, zu, upper], RN.at[a, h, 0, upper], dev_u)
        arrive(("pfd", a, h), RF.at[a, h, 1])
        PS[a, h, zd, lower] += RF[a, h, 1]
        send(("pnd", a, h, 1), PS.at[a, h, zd, lower], RN.at[a, h, 1, lower], dev_d)

    def whole(a, h):
        for n, part in enumerate((lower, upper)):
            arrive(("pnu", a, h, n), RN.at[a, h, 0, part])
        for n, part in enumerate((upper, lower)):
            arrive(("pnd", a, h, n), RN.at[a, h, 1, part])
        return PS[a, h, z] + RN[a, h, 0] + RN[a, h, 1]

    open_x(0)
    open_a(1)
    open_x(1)
    load(1)
    ax(0, 0)
    ax(1, 1)
    open_z(0)
    s1(0)
    s2(0, "")
    s2(0, "x")
    s3(0, "")
    spread(0, 0)
    open_z(1)
    r1(0)
    r3(0, "")
    s3(0, "x")
    r2(0, "x")
    r2(0, "")
    r3(0, "x")
    squares(0)
    ax(0, 1)
    s1(1)
    spread(1, 1)
    spread2(0)
    s2(1, "")
    scale(0)
    s2(1, "x")
    open_a(0)
    r1(1)
    spread(0, 1)
    r2(1, "")
    ax(1, 0)
    s3(1, "")
    r2(1, "x")
    r3(1, "")
    s3(1, "x")
    r3(1, "x")
    squares(1)
    spread3(0)
    sho(0)
    shx(0)
    spread(1, 0)
    scale(1)
    own_ready(0)
    a_ready(0)
    pf(0, 0)
    spread3(1)
    sfar(0)
    pn(0, 0)
    other_ready(0)
    spread2(1)
    pf(0, 1)
    shx(1)
    sho(1)
    own_ready(1)
    pn(0, 1)
    a_ready(1)
    pf(1, 0)
    sfar(1)
    pn(1, 0)
    other_ready(1)
    pf(1, 1)
    pn(1, 1)
    for h in range(2):
        hq = q if h == 0 else p
        PR[pl.ds(hq * rows, rows)] = whole(0, h) * whole(1, h)
    ranks = 32
    pick = (
        lax.broadcasted_iota(jnp.int32, (8, 256), 1) // ranks == lax.broadcasted_iota(jnp.int32, (8, 256), 0)
    ).astype(jnp.float32).astype(jnp.bfloat16)
    left, total = PR[...], None
    for _ in range(3):
        term = left.astype(jnp.bfloat16)
        left = left - term.astype(jnp.float32)
        part = lax.dot_general(pick, term, NT, preferred_element_type=jnp.float32)
        total = part if total is None else total + part
    SC[w] = total
    steps = [(dx, dz, dc) for dz in (2, 1, 3, 0) for dx in (1, 0) for dc in (0, 1) if dx + dz + dc]
    for dx, dz, dc in steps:
        peer = at(lax.rem(x + dx, 2), lax.rem(z + dz, 4), lax.rem(c + dc, 2))
        send(("sc", dx, dz, dc), SC.at[w], SC.at[w], {"width": peer})
    for dx, dz, dc in steps:
        peer = at(lax.rem(x + dx, 2), lax.rem(z + 4 - dz, 4), lax.rem(c + dc, 2))
        arrive(("sc", dx, dz, dc), SC.at[peer])
    out[...] = SC[...]
    for copy in pending:
        copy.wait_send()
    assert len(keys) <= N_SEM


def on_device(layer_inputs, out_grads, basis_in, basis_out, query_in, query_out):
    total_tokens = layer_inputs.shape[0] * lax.axis_size("token") * lax.axis_size("query")
    rows, cols = layer_inputs.shape
    f32, bf16 = jnp.float32, jnp.bfloat16
    hbm = pl.BlockSpec(memory_space=pl.ANY)
    scores = pl.pallas_call(
        lambda *refs: kernel(total_tokens, *refs),
        out_shape=pltpu.VMEM((16, 8, 2 * rows), f32),
        in_specs=[hbm] * 6,
        out_specs=pl.BlockSpec(memory_space=pltpu.VMEM),
        scratch_shapes=[
            pltpu.VMEM((2, 16, rows, cols), bf16),
            pltpu.VMEM((2, 16, cols, cols), bf16),
            pltpu.VMEM((2, 4, 4, 256, cols), bf16),
            pltpu.VMEM((2, rows, cols), f32),
            pltpu.VMEM((2, 8, 8, cols), f32),
            pltpu.VMEM((2, 2, 4, 2 * rows, cols), bf16),
            pltpu.VMEM((2, 2, 4, rows, 256), f32),
            pltpu.VMEM((2, 2, 2, rows // 2, 256), f32),
            pltpu.VMEM((2, 2, 2, rows, 256), f32),
            pltpu.VMEM((2 * rows, 256), f32),
            pltpu.VMEM((16, 8, 2 * rows), f32),
            pltpu.SemaphoreType.DMA((N_SEM,)),
            pltpu.SemaphoreType.DMA((N_SEM,)),
            pltpu.SemaphoreType.DMA((2,)),
            pltpu.SemaphoreType.DMA((2, 8)),
            pltpu.SemaphoreType.DMA((2,)),
        ],
        compiler_params=pltpu.CompilerParams(
            collective_id=0, has_side_effects=True, vmem_limit_bytes=60 * 1024 * 1024
        ),
        name="influence",
    )(
        layer_inputs,
        out_grads,
        basis_in.reshape(16, cols, cols),
        basis_out.reshape(16, cols, cols),
        query_in.reshape(2, 4, 2, 256, cols),
        query_out.reshape(2, 4, 2, 256, cols),
    )
    return scores.reshape(128, 2 * rows)


def solution(mesh):
    return jax.shard_map(
        on_device,
        mesh=mesh,
        in_specs=(
            P(("token", "query"), "width"),
            P(("token", "query"), "width"),
            P(None, "width"),
            P(None, "width"),
            P("query", None, "width"),
            P("query", None, "width"),
        ),
        out_specs=P("query", "token"),
        check_vma=False,
    )
```

```python
import jax
import jax.numpy as jnp
from jax import lax
from jax.experimental import pallas as pl
from jax.experimental.pallas import tpu as pltpu
from jax.sharding import PartitionSpec as P

damping = 0.1
MESH = pl.DeviceIdType.MESH
N_SEM = 160
SPLIT = (False, True)
NT = (((1,), (1,)), ((), ()))


def kernel(total_tokens, li, og, bi, bo, qi, qo, out, X, BAS, A, ACC, AR, S, PS, RF, RN, PR, SC, ss, rs, lx, lb, la):
    acts, bases, queries = (li, og), (bi, bo), (qi, qo)
    w, t, q = lax.axis_index("width"), lax.axis_index("token"), lax.axis_index("query")
    x, z, c = w // 8, lax.rem(w // 2, 4), lax.rem(w, 2)
    xq, cq = 1 - x, 1 - c
    zu, zd, zf = lax.rem(z + 1, 4), lax.rem(z + 3, 4), lax.rem(z + 2, 4)
    tu, td, tf = lax.rem(t + 1, 4), lax.rem(t + 3, 4), lax.rem(t + 2, 4)

    def at(px, pz, pc):
        return (px * 4 + pz) * 2 + pc

    dev_x, dev_c = {"width": at(xq, z, c)}, {"width": at(x, z, cq)}
    dev_u, dev_d = {"width": at(x, zu, c)}, {"width": at(x, zd, c)}
    dev_o = {"width": at(xq, z, c), "query": 1 - q}
    dev_tu, dev_td = {"token": tu}, {"token": td}
    half = X.shape[2] // 2
    rows = X.shape[2]
    upper, lower = pl.ds(0, half), pl.ds(half, half)

    keys, pending = {}, []

    def number(key):
        return keys.setdefault(key, len(keys))

    def send(key, src, dst, dev):
        i = number(key)
        copy = pltpu.make_async_remote_copy(
            src_ref=src, dst_ref=dst, send_sem=ss.at[i], recv_sem=rs.at[i], device_id=dev, device_id_type=MESH
        )
        copy.start()
        pending.append(copy)

    def arrive(key, region, dev=None):
        i = number(key)
        pltpu.make_async_remote_copy(
            src_ref=region, dst_ref=region, send_sem=ss.at[i], recv_sem=rs.at[i],
            device_id=dev_c if dev is None else dev, device_id_type=MESH,
        ).wait_recv()

    me = at(x, z, c)
    own_x = [pltpu.make_async_copy(acts[a], X.at[a, me], lx.at[a]) for a in range(2)]
    for cp in own_x:
        cp.start()
    order = [(x, z), (xq, z), (x, zd), (x, zu), (xq, zd), (xq, zu), (x, zf), (xq, zf)]
    base_copies = {}
    for a in range(2):
        for n, (px, pz) in enumerate(order):
            pair = pl.ds((px * 4 + pz) * 2, 2)
            base_copies[a, n] = pltpu.make_async_copy(bases[a].at[pair], BAS.at[a, pair], lb.at[a, n])
    src_me = x * 2 + c
    own_a = [pltpu.make_async_copy(queries[a].at[x, :, c], A.at[a, src_me], la.at[a]) for a in range(2)]

    def load(a):
        for n in range(8):
            base_copies[a, n].start()

    load(0)
    barrier = pltpu.get_barrier_semaphore()
    met = 0
    for d in range(1, 16):
        pl.semaphore_signal(barrier, inc=1, device_id={"width": lax.rem(w + d, 16)}, device_id_type=MESH)
        met += 1
    eight = t * 2 + q
    mates = []
    for d in range(1, 8):
        m = lax.rem(eight + d, 8)
        mates.append((m, {"token": m // 2, "query": lax.rem(m, 2)}))
        pl.semaphore_signal(barrier, inc=1, device_id=mates[-1][1], device_id_type=MESH)
        met += 1
    pl.semaphore_signal(barrier, inc=1, device_id=dev_o, device_id_type=MESH)
    met += 1
    pl.semaphore_wait(barrier, met)

    done_pairs = [0, 0]

    def rotate(a, n):
        base_copies[a, n].wait()
        px, pz = order[n]
        first = (px * 4 + pz) * 2
        for col in range(0, 512, 256):
            cols = pl.ds(col, 256)
            part = jnp.dot(X[a, first], BAS[a, first, :, cols], preferred_element_type=jnp.float32)
            part += jnp.dot(X[a, first + 1], BAS[a, first + 1, :, cols], preferred_element_type=jnp.float32)
            if done_pairs[a]:
                part += ACC[a, :, cols]
            ACC[a, :, cols] = part
        done_pairs[a] += 1

    def open_x(a):
        own_x[a].wait()
        send(("x", a), X.at[a, me], X.at[a, me], dev_x)
        send(("c", a), X.at[a, me], X.at[a, me], dev_c)

    def open_z(a):
        send(("zu", a), X.at[a, me], X.at[a, me], dev_u)
        send(("zd", a), X.at[a, me], X.at[a, me], dev_d)

    def from_core(key, a, px, pz):
        arrive(key, X.at[a, at(px, pz, cq)])

    def to_core(key, a, px, pz):
        blk = X.at[a, at(px, pz, c)]
        send(key, blk, blk, dev_c)

    def s1(a):
        blk = X.at[a, at(xq, z, c)]
        arrive(("x", a), blk)
        send(("xzu", a), blk, blk, dev_u)
        send(("xzd", a), blk, blk, dev_d)
        to_core(("cx", a), a, xq, z)

    def r1(a):
        from_core(("c", a), a, x, z)
        rotate(a, 0)
        from_core(("cx", a), a, xq, z)
        rotate(a, 1)

    def s2(a, tag):
        px = xq if tag else x
        up, down = at(px, zd, c), at(px, zu, c)
        arrive((tag + "zu", a), X.at[a, up])
        send((tag + "fu", a), X.at[a, up, upper], X.at[a, up, upper], dev_u)
        to_core((tag + "czu", a), a, px, zd)
        arrive((tag + "zd", a), X.at[a, down])
        send((tag + "fd", a), X.at[a, down, lower], X.at[a, down, lower], dev_d)
        to_core((tag + "czd", a), a, px, zu)

    def r2(a, tag):
        px, n = (xq, 4) if tag else (x, 2)
        from_core((tag + "czu", a), a, px, zd)
        rotate(a, n)
        from_core((tag + "czd", a), a, px, zu)
        rotate(a, n + 1)

    def s3(a, tag):
        px = xq if tag else x
        far = at(px, zf, c)
        arrive((tag + "fu", a), X.at[a, far, upper])
        arrive((tag + "fd", a), X.at[a, far, lower])
        to_core((tag + "cf", a), a, px, zf)

    def r3(a, tag):
        px, n = (xq, 7) if tag else (x, 6)
        from_core((tag + "cf", a), a, px, zf)
        rotate(a, n)

    def squares(a):
        val = ACC[a]
        AR[a, eight] = jnp.sum((val * val).reshape(rows // 8, 8, 512), axis=0)
        for d, (m, dev) in enumerate(mates):
            send(("ar", a, d), AR.at[a, eight], AR.at[a, eight], dev)

    def scale(a):
        for d in range(7):
            arrive(("ar", a, d), AR.at[a, lax.rem(eight + 7 - d, 8)])
        tot = AR[a, 0]
        for k in range(1, 8):
            tot += AR[a, k]
        inv = 1.0 / (jnp.sum(tot, axis=0, keepdims=True) / total_tokens + damping)
        val = ACC[a] * inv
        hi = val.astype(jnp.bfloat16)
        S[a, q, src_me, pl.ds(0, rows)] = hi
        S[a, q, src_me, pl.ds(rows, rows)] = (val - hi.astype(jnp.float32)).astype(jnp.bfloat16)
        blk = S.at[a, q, src_me]
        send(("bx", a), blk, blk, dev_x)
        send(("bo", a), blk, blk, dev_o)
        send(("bc", a), blk, blk, dev_c)

    p = 1 - q

    his, los = pl.ds(0, rows), pl.ds(rows, rows)

    def shx(a):
        blk = S.at[a, q, xq * 2 + c]
        arrive(("bx", a), blk)
        part = blk if not SPLIT[a] else S.at[a, q, xq * 2 + c, his]
        send(("bh", a), part, part, dev_o)
        send(("bcx", a), blk, blk, dev_c)

    def sho(a):
        blk = S.at[a, p, xq * 2 + c]
        arrive(("bo", a), blk)
        if SPLIT[a]:
            part = S.at[a, p, xq * 2 + c, los]
            send(("bl", a), part, part, dev_x)
        send(("bco", a), blk, blk, dev_c)

    def sfar(a):
        blk = S.at[a, p, x * 2 + c]
        if SPLIT[a]:
            arrive(("bh", a), S.at[a, p, x * 2 + c, his])
            arrive(("bl", a), S.at[a, p, x * 2 + c, los])
        else:
            arrive(("bh", a), blk)
        send(("bcf", a), blk, blk, dev_c)

    def own_ready(a):
        arrive(("bc", a), S.at[a, q, x * 2 + cq])
        arrive(("bcx", a), S.at[a, q, xq * 2 + cq])

    def other_ready(a):
        arrive(("bco", a), S.at[a, p, xq * 2 + cq])
        arrive(("bcf", a), S.at[a, p, x * 2 + cq])

    def open_a(a):
        own_a[a].start()
        send(("ac", a), queries[a].at[x, :, cq], A.at[a, src_me], dev_c)

    def ax(a, k):
        pc = c if k == 0 else cq
        send(("ax", a, k), queries[a].at[xq, t, pc], A.at[a, src_me, t], {"width": at(xq, z, pc)})

    def spread(a, k):
        pc = c if k == 0 else cq
        blk = A.at[a, xq * 2 + pc, t]
        arrive(("ax", a, k), blk)
        send(("ayu", a, k), blk, blk, dev_tu)
        send(("ayd", a, k), blk, blk, dev_td)

    def spread2(a):
        blk = A.at[a, xq * 2 + c, td]
        arrive(("ayu", a, 0), blk)
        send(("agu", a), blk, blk, dev_tu)

    def spread3(a):
        blk = A.at[a, xq * 2 + cq, tu]
        arrive(("ayd", a, 1), blk)
        send(("agd", a), blk, blk, dev_td)

    def a_ready(a):
        own_a[a].wait()
        arrive(("ac", a), A.at[a, x * 2 + cq])
        arrive(("ayu", a, 1), A.at[a, xq * 2 + cq, td])
        arrive(("ayd", a, 0), A.at[a, xq * 2 + c, tu])
        arrive(("agu", a), A.at[a, xq * 2 + c, tf])
        arrive(("agd", a), A.at[a, xq * 2 + cq, tf])

    def pair(a, h, zz):
        hq = q if h == 0 else p
        acc = None
        for k in range(4):
            part = lax.dot_general(S[a, hq, k], A[a, k, zz], NT, preferred_element_type=jnp.float32)
            acc = part if acc is None else acc + part
        PS[a, h, zz] = acc[:rows] + acc[rows:]

    def pf(a, h):
        pair(a, h, zf)
        send(("pfu", a, h), PS.at[a, h, zf, upper], RF.at[a, h, 0], dev_u)
        send(("pfd", a, h), PS.at[a, h, zf, lower], RF.at[a, h, 1], dev_d)
        pair(a, h, zu)
        send(("pnu", a, h, 0), PS.at[a, h, zu, lower], RN.at[a, h, 0, lower], dev_u)
        pair(a, h, zd)
        send(("pnd", a, h, 0), PS.at[a, h, zd, upper], RN.at[a, h, 1, upper], dev_d)
        pair(a, h, z)

    def pn(a, h):
        arrive(("pfu", a, h), RF.at[a, h, 0])
        PS[a, h, zu, upper] += RF[a, h, 0]
        send(("pnu", a, h, 1), PS.at[a, h, zu, upper], RN.at[a, h, 0, upper], dev_u)
        arrive(("pfd", a, h), RF.at[a, h, 1])
        PS[a, h, zd, lower] += RF[a, h, 1]
        send(("pnd", a, h, 1), PS.at[a, h, zd, lower], RN.at[a, h, 1, lower], dev_d)

    def whole(a, h):
        for n, part in enumerate((lower, upper)):
            arrive(("pnu", a, h, n), RN.at[a, h, 0, part])
        for n, part in enumerate((upper, lower)):
            arrive(("pnd", a, h, n), RN.at[a, h, 1, part])
        return PS[a, h, z] + RN[a, h, 0] + RN[a, h, 1]

    open_x(0)
    open_x(1)
    ax(0, 0)
    ax(0, 1)
    open_z(0)
    s1(0)
    load(1)
    s2(0, "")
    s2(0, "x")
    s3(0, "")
    spread(0, 0)
    open_z(1)
    r1(0)
    r3(0, "")
    s3(0, "x")
    r2(0, "x")
    r2(0, "")
    r3(0, "x")
    squares(0)
    ax(1, 1)
    s1(1)
    spread(0, 1)
    spread2(0)
    s2(1, "")
    scale(0)
    s2(1, "x")
    open_a(0)
    r1(1)
    spread(1, 1)
    r2(1, "")
    ax(1, 0)
    s3(1, "")
    r2(1, "x")
    r3(1, "")
    s3(1, "x")
    r3(1, "x")
    squares(1)
    open_a(1)
    spread3(0)
    sho(0)
    shx(0)
    spread(1, 0)
    scale(1)
    own_ready(0)
    a_ready(0)
    pf(0, 0)
    spread3(1)
    sfar(0)
    pn(0, 0)
    other_ready(0)
    spread2(1)
    pf(0, 1)
    shx(1)
    sho(1)
    own_ready(1)
    pn(0, 1)
    a_ready(1)
    pf(1, 0)
    sfar(1)
    pn(1, 0)
    other_ready(1)
    pf(1, 1)
    pn(1, 1)
    for h in range(2):
        hq = q if h == 0 else p
        PR[pl.ds(hq * rows, rows)] = whole(0, h) * whole(1, h)
    ranks = 32
    pick = (
        lax.broadcasted_iota(jnp.int32, (8, 256), 1) // ranks == lax.broadcasted_iota(jnp.int32, (8, 256), 0)
    ).astype(jnp.float32).astype(jnp.bfloat16)
    left, total = PR[...], None
    for _ in range(3):
        term = left.astype(jnp.bfloat16)
        left = left - term.astype(jnp.float32)
        part = lax.dot_general(pick, term, NT, preferred_element_type=jnp.float32)
        total = part if total is None else total + part
    SC[w] = total
    steps = [(dx, dz, dc) for dz in (2, 1, 3, 0) for dx in (1, 0) for dc in (0, 1) if dx + dz + dc]
    for dx, dz, dc in steps:
        peer = at(lax.rem(x + dx, 2), lax.rem(z + dz, 4), lax.rem(c + dc, 2))
        send(("sc", dx, dz, dc), SC.at[w], SC.at[w], {"width": peer})
    for dx, dz, dc in steps:
        peer = at(lax.rem(x + dx, 2), lax.rem(z + 4 - dz, 4), lax.rem(c + dc, 2))
        arrive(("sc", dx, dz, dc), SC.at[peer])
    out[...] = SC[...]
    for copy in pending:
        copy.wait_send()
    assert len(keys) <= N_SEM


def on_device(layer_inputs, out_grads, basis_in, basis_out, query_in, query_out):
    total_tokens = layer_inputs.shape[0] * lax.axis_size("token") * lax.axis_size("query")
    rows, cols = layer_inputs.shape
    f32, bf16 = jnp.float32, jnp.bfloat16
    hbm = pl.BlockSpec(memory_space=pl.ANY)
    scores = pl.pallas_call(
        lambda *refs: kernel(total_tokens, *refs),
        out_shape=pltpu.VMEM((16, 8, 2 * rows), f32),
        in_specs=[hbm] * 6,
        out_specs=pl.BlockSpec(memory_space=pltpu.VMEM),
        scratch_shapes=[
            pltpu.VMEM((2, 16, rows, cols), bf16),
            pltpu.VMEM((2, 16, cols, cols), bf16),
            pltpu.VMEM((2, 4, 4, 256, cols), bf16),
            pltpu.VMEM((2, rows, cols), f32),
            pltpu.VMEM((2, 8, 8, cols), f32),
            pltpu.VMEM((2, 2, 4, 2 * rows, cols), bf16),
            pltpu.VMEM((2, 2, 4, rows, 256), f32),
            pltpu.VMEM((2, 2, 2, rows // 2, 256), f32),
            pltpu.VMEM((2, 2, 2, rows, 256), f32),
            pltpu.VMEM((2 * rows, 256), f32),
            pltpu.VMEM((16, 8, 2 * rows), f32),
            pltpu.SemaphoreType.DMA((N_SEM,)),
            pltpu.SemaphoreType.DMA((N_SEM,)),
            pltpu.SemaphoreType.DMA((2,)),
            pltpu.SemaphoreType.DMA((2, 8)),
            pltpu.SemaphoreType.DMA((2,)),
        ],
        compiler_params=pltpu.CompilerParams(
            collective_id=0, has_side_effects=True, vmem_limit_bytes=60 * 1024 * 1024
        ),
        name="influence",
    )(
        layer_inputs,
        out_grads,
        basis_in.reshape(16, cols, cols),
        basis_out.reshape(16, cols, cols),
        query_in.reshape(2, 4, 2, 256, cols),
        query_out.reshape(2, 4, 2, 256, cols),
    )
    return scores.reshape(128, 2 * rows)


def solution(mesh):
    return jax.shard_map(
        on_device,
        mesh=mesh,
        in_specs=(
            P(("token", "query"), "width"),
            P(("token", "query"), "width"),
            P(None, "width"),
            P(None, "width"),
            P("query", None, "width"),
            P("query", None, "width"),
        ),
        out_specs=P("query", "token"),
        check_vma=False,
    )
```
